32 devices in a mesh: cuts: 2 (over x), outer: 16 (over z, y, core).
Axes of the slice: x: 2, y: 2, z: 4, core: 2. Of those that a mesh axis runs over, the one named last changes fastest.
Arguments:
- stem_tensor: bfloat16 [32, 512, 2, 512], P(('cuts', 'outer')), parts along dimension 0, may hold values from -6 to 6
- leaf_left: bfloat16 [4, 2, 8192, 2, 512], P(None, None, 'outer'), may hold values from -0.09375 to 0.09375
- leaf_right: bfloat16 [4, 2, 8192, 2, 512], P(None, None, 'outer'), may hold values from -0.125 to 0.125
- slice_bits: int32 [8], P('cuts'), parts along dimension 0, may hold values from 0 to 1, as said below
Outputs:
- stem_out: bfloat16 [32, 512, 2, 512], P(('cuts', 'outer')), parts along dimension 0
The draws below stay inside these ranges and needn't reach their ends.
There are 2 independent parts, one for each index of `cuts`. The reference program is written for one: setup_inputs(seed, part) draws one part's arguments, and reference() takes and returns one part's arrays. A program takes and returns all parts, laid end to end along the dimension named above; an argument that names none is the same for every part. Nothing has to cross between parts.
Inputs may be any that keep to these rules, and one draw needn't show every extreme that they name: `slice_bits`: the first entry is the index of the part modulo 2, so neighbouring parts contract different slices; the other entries are drawn independently.
All inputs are finite; a program needn't handle non-finite values.
Results may differ from the reference program's by a relative error of at most 0.01.
Values may be sent and summed in bfloat16 or wider, within the bound.
A program may use at most 64 MiB of HBM per device.

```python
import jax
import jax.numpy as jnp
from jax import lax

W = 512
K = 8192
ROUNDS = 2
SLICES = 2
BR = 4
SHARDS = 16


def draw_slice_bits(key, part):
    drawn = jax.random.randint(key, (BR,), 0, 2, dtype=jnp.int32)
    first = jnp.asarray(part, jnp.int32) % 2
    return drawn.at[0].set(first)


def with_spikes(entries, own_key, source, target, blocks, factor):
    def block_of(axis_at):
        return (jnp.arange(entries.shape[axis_at]) // (entries.shape[axis_at] // blocks)).reshape((-1,) + (1,) * (entries.ndim - 1 - axis_at))

    one_side = jax.random.permutation(own_key, blocks)[block_of(target)]
    other_side = (block_of(target) + blocks // 2) % blocks
    return jnp.where((block_of(source) == one_side) | (block_of(source) == other_side), factor * entries, entries)


def levels(key, dims, pieces, low, largest):
    gain, own = 1.0, jax.random.fold_in(key, 6)
    for dim, blocks in pieces:
        steps = jnp.exp(jax.random.uniform(jax.random.fold_in(own, dim), (blocks,), jnp.float32, low / len(pieces), largest / len(pieces)))
        gain = gain * jnp.repeat(steps, dims[dim] // blocks).reshape([-1 if axis == dim else 1 for axis in range(len(dims))])
    return gain


def gaussian(stream_key, extent, scale, reach, cuts=(), kind=jnp.bfloat16):
    values = scale * jax.random.normal(stream_key, extent, jnp.float32)
    if cuts:
        values = values * levels(stream_key, extent, cuts, -0.22, 0.18)
    return jnp.clip(values, -reach, reach).astype(kind)


def bell_draw_with(own_key, shape, width, most, cuts, heavy, kind=jnp.bfloat16):
    values = width * jax.random.normal(own_key, shape, jnp.float32)
    if cuts:
        values = values * levels(own_key, shape, cuts, -0.22, 0.18)
    return jnp.clip(with_spikes(values, jax.random.fold_in(own_key, 3), *heavy), -most, most).astype(kind)


def setup_inputs(seed: int = 0, part: int = 0) -> dict:
    keys = jax.random.split(jax.random.key(seed), 5)
    part_splits = jax.random.split(jax.random.fold_in(keys[4], part), 5)
    stem_tensor = gaussian(part_splits[0], (SHARDS, W, 2, W), 1.0, 6.0, ((0, 16),))
    leaf_left = bell_draw_with(keys[1], (BR, SLICES, K, 2, W), K ** -0.5, 0.09375, ((2, 16),), (2, 4, 16, 2.0))
    leaf_right = gaussian(keys[2], (BR, SLICES, K, 2, W), (4 * W) ** -0.5, 0.125, ((2, 16),))
    slice_bits = draw_slice_bits(jax.random.fold_in(jax.random.fold_in(keys[4], part), 71), part)
    return {"stem_tensor": stem_tensor, "leaf_left": leaf_left, "leaf_right": leaf_right, "slice_bits": slice_bits}


def complex_leaves(left_leaf, right_leaf):
    product = jnp.einsum('kpi,kqm->piqm', left_leaf, right_leaf)
    real_part = product[0, :, 0] - product[1, :, 1]
    imag_part = product[0, :, 1] + product[1, :, 0]
    return jnp.stack([real_part, imag_part], axis=1)


def reference(stem_tensor, leaf_left, leaf_right, slice_bits):
    branches = []
    for branch_index in range(2 * ROUNDS):
        chosen = slice_bits[branch_index].astype(jnp.int32)
        left_leaf = lax.dynamic_index_in_dim(leaf_left[branch_index], chosen, 0, keepdims=False).astype(jnp.float32)
        right_leaf = lax.dynamic_index_in_dim(leaf_right[branch_index], chosen, 0, keepdims=False).astype(jnp.float32)
        branches.append(complex_leaves(left_leaf, right_leaf).astype(jnp.bfloat16))
    shards = SHARDS
    span = W // SHARDS
    state = stem_tensor
    for round_index in range(ROUNDS):
        p_branch = branches[2 * round_index].astype(jnp.float32)
        q_branch = branches[2 * round_index + 1].astype(jnp.float32)
        current = state.astype(jnp.float32)
        product = jnp.einsum('abpc,cqm->abpqm', current, q_branch)
        real_part = product[:, :, 0, 0] - product[:, :, 1, 1]
        imag_part = product[:, :, 0, 1] + product[:, :, 1, 0]
        absorbed = jnp.stack([real_part, imag_part], axis=2).astype(jnp.bfloat16)
        grouped = absorbed.astype(jnp.float32).reshape(shards, shards, span, 2, W)
        p_grouped = p_branch.reshape(shards, span, 2, W)
        product = jnp.einsum('ahlpm,alqn->hnpqm', grouped, p_grouped)
        real_part = product[:, :, 0, 0] - product[:, :, 1, 1]
        imag_part = product[:, :, 0, 1] + product[:, :, 1, 0]
        state = jnp.stack([real_part, imag_part], axis=2).astype(jnp.bfloat16)
    return state
```

```python
import functools

import jax
import jax.numpy as jnp
from jax import lax
from jax.experimental import pallas as pl
from jax.experimental.pallas import tpu as pltpu
from jax.sharding import PartitionSpec as P

ROUNDS = 2
CHUNKS = 4
MESH = pl.DeviceIdType.MESH


def exchange_kernel(n, part, blocks, out, got, acc, outgoing, incoming, a_send, a_recv, r_send, r_recv):
    chunks = part.shape[0]
    steps = n.bit_length() - 1
    me = lax.axis_index("outer")

    barrier = pltpu.get_barrier_semaphore()

    def greet(k, carry):
        pl.semaphore_signal(barrier, inc=1, device_id={"outer": lax.rem(me + k, n)}, device_id_type=MESH)
        return carry

    lax.fori_loop(1, n, greet, 0)
    pl.semaphore_wait(barrier, n - 1)

    bits = [lax.rem(me // (1 << s), 2) for s in range(steps)]
    peers = [me + (1 << s) * (1 - 2 * bits[s]) for s in range(steps)]
    starts = [0]
    gives = []
    for s in range(steps):
        half = n >> (s + 1)
        gives.append(starts[s] + (1 - bits[s]) * half)
        starts.append(starts[s] + bits[s] * half)

    def move(k):
        to = lax.rem(me + k, n)
        return pltpu.make_async_remote_copy(
            src_ref=blocks.at[to], dst_ref=got.at[me], send_sem=a_send.at[k], recv_sem=a_recv.at[k],
            device_id={"outer": to}, device_id_type=MESH)

    def arrival(k):
        origin = lax.rem(me + n - k, n)
        return pltpu.make_async_remote_copy(
            src_ref=blocks.at[origin], dst_ref=got.at[origin], send_sem=a_send.at[k], recv_sem=a_recv.at[k],
            device_id={"outer": origin}, device_id_type=MESH)

    def reduce_copy(c, s):
        half, at = n >> (s + 1), n - (n >> s)
        return pltpu.make_async_remote_copy(
            src_ref=outgoing.at[c, pl.ds(gives[s], half)], dst_ref=incoming.at[c, pl.ds(at, half)],
            send_sem=r_send.at[c, s], recv_sem=r_recv.at[c, s],
            device_id={"outer": peers[s]}, device_id_type=MESH)

    def gather_copy(c, s, first):
        half = n >> (s + 1)
        here = out.at[c, pl.ds(first, half)]
        return pltpu.make_async_remote_copy(
            src_ref=here, dst_ref=here, send_sem=r_send.at[c, 2 * steps - 1 - s], recv_sem=r_recv.at[c, 2 * steps - 1 - s],
            device_id={"outer": peers[s]}, device_id_type=MESH)

    def begin(c, step):
        if step < steps:
            half = n >> (step + 1)
            source = part if step == 0 else acc
            give = pl.ds(gives[step], half)
            outgoing[c, give] = source[c, give].astype(outgoing.dtype)
            reduce_copy(c, step).start()
        else:
            s = 2 * steps - 1 - step
            gather_copy(c, s, starts[s + 1]).start()

    def finish(c, step):
        if step < steps:
            half, at = n >> (step + 1), n - (n >> step)
            reduce_copy(c, step).wait_recv()
            source = part if step == 0 else acc
            keep = pl.ds(starts[step + 1], half)
            total = source[c, keep] + incoming[c, pl.ds(at, half)].astype(jnp.float32)
            if step == steps - 1:
                out[c, keep] = total.astype(out.dtype)
            else:
                acc[c, keep] = total
        else:
            s = 2 * steps - 1 - step
            gather_copy(c, s, gives[s]).wait_recv()

    slots = chunks + 2 * steps
    sent = 1
    for t in range(slots):
        for c in range(chunks):
            step = t - c
            if 1 <= step <= 2 * steps:
                finish(c, step - 1)
            if 0 <= step < 2 * steps:
                begin(c, step)
        upto = min(n, 1 + -(-(n - 1) * (t + 1) // max(1, slots - 3)))

        def launch(k, carry):
            move(k).start()
            return carry

        if upto > sent:
            lax.fori_loop(sent, upto, launch, 0)
            sent = upto
    got[me] = blocks[me]

    def settle(k, carry):
        arrival(k).wait_recv()
        move(k).wait_send()
        return carry

    lax.fori_loop(1, n, settle, 0)
    for c in range(chunks):
        for s in range(steps):
            reduce_copy(c, s).wait_send()
            gather_copy(c, s, starts[s + 1]).wait_send()


def exchange(n, part, blocks, call):
    chunks, steps = part.shape[0], n.bit_length() - 1
    vmem = pl.BlockSpec(memory_space=pltpu.VMEM)
    return pl.pallas_call(
        functools.partial(exchange_kernel, n),
        out_shape=(
            jax.ShapeDtypeStruct(part.shape, jnp.bfloat16),
            jax.ShapeDtypeStruct(blocks.shape, blocks.dtype),
        ),
        in_specs=[vmem, vmem],
        out_specs=(vmem, vmem),
        scratch_shapes=[
            pltpu.VMEM(part.shape, jnp.float32),
            pltpu.VMEM(part.shape, jnp.bfloat16),
            pltpu.VMEM(part.shape, jnp.bfloat16),
            pltpu.SemaphoreType.DMA((n,)),
            pltpu.SemaphoreType.DMA((n,)),
            pltpu.SemaphoreType.DMA((chunks, 2 * steps)),
            pltpu.SemaphoreType.DMA((chunks, 2 * steps)),
        ],
        compiler_params=pltpu.CompilerParams(collective_id=call, has_side_effects=True),
    )(part, blocks)


def leaf_term(left_leaf, right_leaf):
    depth, _, row_count = left_leaf.shape
    width = right_leaf.shape[2]
    product = lax.dot_general(
        left_leaf.reshape(depth, 2 * row_count),
        right_leaf.reshape(depth, 2 * width),
        (((0,), (0,)), ((), ())),
        preferred_element_type=jnp.float32,
    )
    product = product.reshape(2, row_count, 2, width)
    real_part = product[0, :, 0] - product[1, :, 1]
    imag_part = product[0, :, 1] + product[1, :, 0]
    return jnp.stack([real_part, imag_part], axis=0)


def complex_product(left, right, dims):
    def dot(a, b):
        return lax.dot_general(a, b, (dims, ((), ())), preferred_element_type=jnp.float32)

    real_part = dot(left[0], right[0]) - dot(left[1], right[1])
    imag_part = dot(left[0], right[1]) + dot(left[1], right[0])
    return jnp.stack([real_part, imag_part], axis=0).astype(jnp.bfloat16)


def on_device(n, stem_tensor, leaf_left, leaf_right, slice_bits):
    width, columns = stem_tensor.shape[1], stem_tensor.shape[3]
    span = width // n
    state = jnp.transpose(stem_tensor[0], (1, 0, 2))
    parts = []
    for branch_index in range(2 * ROUNDS):
        chosen = slice_bits[branch_index]
        parts.append(
            leaf_term(
                lax.dynamic_index_in_dim(leaf_left[branch_index], chosen, 0, keepdims=False),
                lax.dynamic_index_in_dim(leaf_right[branch_index], chosen, 0, keepdims=False),
            )
        )
    for r in range(ROUNDS):
        part = jnp.stack(parts[2 * r : 2 * r + 2])
        part = part.reshape(CHUNKS, n, -1, columns)
        blocks = jnp.transpose(state.reshape(2, n, span, columns), (1, 0, 2, 3)).reshape(n, 2 * span, columns)
        branches, got = exchange(n, part, blocks, r)
        branches = branches.reshape(2, 2, width, columns)
        regrouped = jnp.transpose(got.reshape(n, 2, span, columns), (1, 0, 2, 3)).reshape(2, width, columns)
        absorbed = complex_product(regrouped, branches[1], ((1,), (0,)))
        state = complex_product(branches[0], absorbed, ((0,), (0,)))
    return jnp.transpose(state, (1, 0, 2))[None]


def solution(mesh):
    return jax.shard_map(
        functools.partial(on_device, mesh.shape["outer"]),
        mesh=mesh,
        in_specs=(
            P(("cuts", "outer"), None, None, None),
            P(None, None, "outer", None, None),
            P(None, None, "outer", None, None),
            P("cuts"),
        ),
        out_specs=P(("cuts", "outer"), None, None, None),
        check_vma=False,
    )
```

```python
import functools

import jax
import jax.numpy as jnp
from jax import lax
from jax.experimental import pallas as pl
from jax.experimental.pallas import tpu as pltpu
from jax.sharding import PartitionSpec as P

ROUNDS = 2
CHUNKS = 4
MESH = pl.DeviceIdType.MESH


def exchange_kernel(n, part, blocks, out, got, acc, outgoing, incoming, a_send, a_recv, r_send, r_recv):
    chunks = part.shape[0]
    steps = n.bit_length() - 1
    me = lax.axis_index("outer")

    barrier = pltpu.get_barrier_semaphore()

    def greet(k, carry):
        pl.semaphore_signal(barrier, inc=1, device_id={"outer": lax.rem(me + k, n)}, device_id_type=MESH)
        return carry

    lax.fori_loop(1, n, greet, 0)
    pl.semaphore_wait(barrier, n - 1)

    bits = [lax.rem(me // (1 << s), 2) for s in range(steps)]
    peers = [me + (1 << s) * (1 - 2 * bits[s]) for s in range(steps)]
    starts = [0]
    gives = []
    for s in range(steps):
        half = n >> (s + 1)
        gives.append(starts[s] + (1 - bits[s]) * half)
        starts.append(starts[s] + bits[s] * half)

    def move(k):
        to = lax.rem(me + k, n)
        return pltpu.make_async_remote_copy(
            src_ref=blocks.at[to], dst_ref=got.at[me], send_sem=a_send.at[k], recv_sem=a_recv.at[k],
            device_id={"outer": to}, device_id_type=MESH)

    def arrival(k):
        origin = lax.rem(me + n - k, n)
        return pltpu.make_async_remote_copy(
            src_ref=blocks.at[origin], dst_ref=got.at[origin], send_sem=a_send.at[k], recv_sem=a_recv.at[k],
            device_id={"outer": origin}, device_id_type=MESH)

    def reduce_copy(c, s):
        half, at = n >> (s + 1), n - (n >> s)
        return pltpu.make_async_remote_copy(
            src_ref=outgoing.at[c, pl.ds(gives[s], half)], dst_ref=incoming.at[c, pl.ds(at, half)],
            send_sem=r_send.at[c, s], recv_sem=r_recv.at[c, s],
            device_id={"outer": peers[s]}, device_id_type=MESH)

    def gather_copy(c, s, first):
        half = n >> (s + 1)
        here = out.at[c, pl.ds(first, half)]
        return pltpu.make_async_remote_copy(
            src_ref=here, dst_ref=here, send_sem=r_send.at[c, 2 * steps - 1 - s], recv_sem=r_recv.at[c, 2 * steps - 1 - s],
            device_id={"outer": peers[s]}, device_id_type=MESH)

    def begin(c, step):
        if step < steps:
            half = n >> (step + 1)
            source = part if step == 0 else acc
            give = pl.ds(gives[step], half)
            outgoing[c, give] = source[c, give].astype(outgoing.dtype)
            reduce_copy(c, step).start()
        else:
            s = 2 * steps - 1 - step
            gather_copy(c, s, starts[s + 1]).start()

    def finish(c, step):
        if step < steps:
            half, at = n >> (step + 1), n - (n >> step)
            reduce_copy(c, step).wait_recv()
            source = part if step == 0 else acc
            keep = pl.ds(starts[step + 1], half)
            total = source[c, keep] + incoming[c, pl.ds(at, half)].astype(jnp.float32)
            if step == steps - 1:
                out[c, keep] = total.astype(out.dtype)
            else:
                acc[c, keep] = total
        else:
            s = 2 * steps - 1 - step
            gather_copy(c, s, gives[s]).wait_recv()

    slots = chunks + 2 * steps
    sent = 1
    for t in range(slots):
        for c in range(chunks):
            step = t - c
            if 1 <= step <= 2 * steps:
                finish(c, step - 1)
            if 0 <= step < 2 * steps:
                begin(c, step)
        upto = min(n, 1 + -(-(n - 1) * (t + 1) // max(1, slots - 3)))

        def launch(k, carry):
            move(k).start()
            return carry

        if upto > sent:
            lax.fori_loop(sent, upto, launch, 0)
            sent = upto
    got[me] = blocks[me]

    def settle(k, carry):
        arrival(k).wait_recv()
        move(k).wait_send()
        return carry

    lax.fori_loop(1, n, settle, 0)
    for c in range(chunks):
        for s in range(steps):
            reduce_copy(c, s).wait_send()
            gather_copy(c, s, starts[s + 1]).wait_send()


def exchange(n, part, blocks, call):
    chunks, steps = part.shape[0], n.bit_length() - 1
    vmem = pl.BlockSpec(memory_space=pltpu.VMEM)
    return pl.pallas_call(
        functools.partial(exchange_kernel, n),
        out_shape=(
            jax.ShapeDtypeStruct(part.shape, jnp.bfloat16),
            jax.ShapeDtypeStruct(blocks.shape, blocks.dtype),
        ),
        in_specs=[vmem, vmem],
        out_specs=(vmem, vmem),
        scratch_shapes=[
            pltpu.VMEM(part.shape, jnp.float32),
            pltpu.VMEM(part.shape, jnp.bfloat16),
            pltpu.VMEM(part.shape, jnp.bfloat16),
            pltpu.SemaphoreType.DMA((n,)),
            pltpu.SemaphoreType.DMA((n,)),
            pltpu.SemaphoreType.DMA((chunks, 2 * steps)),
            pltpu.SemaphoreType.DMA((chunks, 2 * steps)),
        ],
        compiler_params=pltpu.CompilerParams(collective_id=call, has_side_effects=True),
    )(part, blocks)


def leaf_kernel(bits, left_ref, right_ref, out_ref):
    depth, row_count = left_ref.shape[2], left_ref.shape[4]
    width = right_ref.shape[4]
    left = left_ref[0, 0].reshape(2 * depth, row_count)
    right = right_ref[0, 0].reshape(2 * depth, width).astype(jnp.float32)
    even = lax.rem(lax.broadcasted_iota(jnp.int32, right.shape, 0), 2) == 0
    signed = jnp.where(even, right, -right).astype(jnp.bfloat16)
    swapped = jnp.where(even, pltpu.roll(right, 2 * depth - 1, 0), pltpu.roll(right, 1, 0)).astype(jnp.bfloat16)
    dims = (((0,), (0,)), ((), ()))
    out_ref[0, 0] = lax.dot_general(left, signed, dims, preferred_element_type=jnp.float32)
    out_ref[0, 1] = lax.dot_general(left, swapped, dims, preferred_element_type=jnp.float32)


def leaf_terms(bits, leaf_left, leaf_right, first):
    _, _, depth, _, row_count = leaf_left.shape
    width = leaf_right.shape[4]

    def chosen(j, chosen_bits):
        return (first + j, chosen_bits[first + j], 0, 0, 0)

    return pl.pallas_call(
        leaf_kernel,
        out_shape=jax.ShapeDtypeStruct((2, 2, row_count, width), jnp.float32),
        grid_spec=pltpu.PrefetchScalarGridSpec(
            num_scalar_prefetch=1,
            grid=(2,),
            in_specs=[
                pl.BlockSpec((1, 1, depth, 2, row_count), chosen),
                pl.BlockSpec((1, 1, depth, 2, width), chosen),
            ],
            out_specs=pl.BlockSpec((1, 2, row_count, width), lambda j, chosen_bits: (j, 0, 0, 0)),
        ),
    )(bits, leaf_left, leaf_right)


def complex_product(left, right, dims):
    def dot(a, b):
        return lax.dot_general(a, b, (dims, ((), ())), preferred_element_type=jnp.float32)

    real_part = dot(left[0], right[0]) - dot(left[1], right[1])
    imag_part = dot(left[0], right[1]) + dot(left[1], right[0])
    return jnp.stack([real_part, imag_part], axis=0).astype(jnp.bfloat16)


def on_device(n, stem_tensor, leaf_left, leaf_right, slice_bits):
    width, columns = stem_tensor.shape[1], stem_tensor.shape[3]
    span = width // n
    state = jnp.transpose(stem_tensor[0], (1, 0, 2))
    for r in range(ROUNDS):
        part = leaf_terms(slice_bits, leaf_left, leaf_right, 2 * r).reshape(CHUNKS, n, -1, columns)
        blocks = jnp.transpose(state.reshape(2, n, span, columns), (1, 0, 2, 3)).reshape(n, 2 * span, columns)
        branches, got = exchange(n, part, blocks, r)
        branches = branches.reshape(2, 2, width, columns)
        regrouped = jnp.transpose(got.reshape(n, 2, span, columns), (1, 0, 2, 3)).reshape(2, width, columns)
        absorbed = complex_product(regrouped, branches[1], ((1,), (0,)))
        state = complex_product(branches[0], absorbed, ((0,), (0,)))
    return jnp.transpose(state, (1, 0, 2))[None]


def solution(mesh):
    return jax.shard_map(
        functools.partial(on_device, mesh.shape["outer"]),
        mesh=mesh,
        in_specs=(
            P(("cuts", "outer"), None, None, None),
            P(None, None, "outer", None, None),
            P(None, None, "outer", None, None),
            P("cuts"),
        ),
        out_specs=P(("cuts", "outer"), None, None, None),
        check_vma=False,
    )
```

```python
import functools

import jax
import jax.numpy as jnp
from jax import lax
from jax.experimental import pallas as pl
from jax.experimental.pallas import tpu as pltpu
from jax.sharding import PartitionSpec as P

ROUNDS = 2
PLANES = 4
TILES = 4
LAG = 2
EARLY = 4
SPREAD = 0.8
UNITS = 2
MESH = pl.DeviceIdType.MESH


def network_kernel(
    n, part0, part1, blocks0, out, acc, outgoing, incoming, branch, got0, got1, blocks1, absorbed,
    a_send, a_recv, r_send, r_recv,
):
    planes = part0.shape[0]
    chunks = 2 * planes
    span, columns = part0.shape[2], part0.shape[3]
    width = n * span
    steps = n.bit_length() - 1
    tiles = TILES
    group = n // tiles
    me = lax.axis_index("outer")
    high, low = me // group, lax.rem(me, group)

    barrier = pltpu.get_barrier_semaphore()

    def greet(k, carry):
        pl.semaphore_signal(barrier, inc=1, device_id={"outer": lax.rem(me + k, n)}, device_id_type=MESH)
        return carry

    lax.fori_loop(1, n, greet, 0)
    pl.semaphore_wait(barrier, n - 1)

    bits = [lax.rem(me // (1 << s), 2) for s in range(steps)]
    peers = [me + (1 << s) * (1 - 2 * bits[s]) for s in range(steps)]
    starts = [0]
    gives = []
    for s in range(steps):
        half = n >> (s + 1)
        gives.append(starts[s] + (1 - bits[s]) * half)
        starts.append(starts[s] + bits[s] * half)

    def copy_to(r, i, j):
        to = lax.rem(high + i, tiles) * group + lax.rem(low + j, group)
        k = i * group + j
        blocks, got = ((blocks0, got0), (blocks1, got1))[r]
        return pltpu.make_async_remote_copy(
            src_ref=blocks.at[to], dst_ref=got.at[me], send_sem=a_send.at[r, k], recv_sem=a_recv.at[r, k],
            device_id={"outer": to}, device_id_type=MESH)

    def copy_from(r, i, j):
        origin = lax.rem(high + tiles - i, tiles) * group + lax.rem(low + group - j, group)
        k = i * group + j
        blocks, got = ((blocks0, got0), (blocks1, got1))[r]
        return pltpu.make_async_remote_copy(
            src_ref=blocks.at[origin], dst_ref=got.at[origin], send_sem=a_send.at[r, k], recv_sem=a_recv.at[r, k],
            device_id={"outer": origin}, device_id_type=MESH)

    def over(i, act):
        def one(j, carry):
            act(i, j)
            return carry

        lax.fori_loop(1 if i == 0 else 0, group, one, 0)

    def source(c, step):
        if step:
            return acc, c
        return (part0, c) if c < planes else (part1, c - planes)

    def reduce_copy(c, s):
        half, at = n >> (s + 1), n - (n >> s)
        return pltpu.make_async_remote_copy(
            src_ref=outgoing.at[c, pl.ds(gives[s], half)], dst_ref=incoming.at[c, pl.ds(at, half)],
            send_sem=r_send.at[c, s], recv_sem=r_recv.at[c, s],
            device_id={"outer": peers[s]}, device_id_type=MESH)

    def gather_copy(c, s, first):
        here = branch.at[c, pl.ds(first, n >> (s + 1))]
        return pltpu.make_async_remote_copy(
            src_ref=here, dst_ref=here, send_sem=r_send.at[c, 2 * steps - 1 - s], recv_sem=r_recv.at[c, 2 * steps - 1 - s],
            device_id={"outer": peers[s]}, device_id_type=MESH)

    def begin(c, step):
        if step < steps:
            give = pl.ds(gives[step], n >> (step + 1))
            ref, at = source(c, step)
            outgoing[c, give] = ref[at, give].astype(outgoing.dtype)
            reduce_copy(c, step).start()
        else:
            s = 2 * steps - 1 - step
            gather_copy(c, s, starts[s + 1]).start()

    def finish(c, step):
        if step < steps:
            half, at = n >> (step + 1), n - (n >> step)
            reduce_copy(c, step).wait_recv()
            keep = pl.ds(starts[step + 1], half)
            ref, own = source(c, step)
            total = ref[own, keep] + incoming[c, pl.ds(at, half)].astype(jnp.float32)
            if step == steps - 1:
                branch[c, keep] = total.astype(branch.dtype)
            else:
                acc[c, keep] = total
        else:
            s = 2 * steps - 1 - step
            gather_copy(c, s, gives[s]).wait_recv()

    def dot(a, b):
        return jnp.dot(a, b, preferred_element_type=jnp.float32)

    def absorb(r, i):
        got = (got0, got1)[r]
        over(i, lambda i, j: copy_from(r, i, j).wait_recv())
        here = pl.ds(lax.rem(high + tiles - i, tiles) * group, group)
        entries = got[here].reshape(group * 2 * span, columns)
        first = r * planes
        by_real = dot(entries, branch[first + 2].reshape(width, columns)).reshape(group, 2, span, columns)
        by_imag = dot(entries, branch[first + 3].reshape(width, columns)).reshape(group, 2, span, columns)
        absorbed[0, here] = (by_real[:, 0] - by_imag[:, 1]).astype(absorbed.dtype)
        absorbed[1, here] = (by_imag[:, 0] + by_real[:, 1]).astype(absorbed.dtype)

    def contract(r, where):
        here = pl.ds(where * group, group)
        first = r * planes
        p_real = branch[first, here].reshape(group * span, width)
        p_imag = branch[first + 1, here].reshape(group * span, width)
        a_real, a_imag = absorbed[0].reshape(width, columns), absorbed[1].reshape(width, columns)
        real_part = (dot(p_real, a_real) - dot(p_imag, a_imag)).astype(jnp.bfloat16)
        imag_part = (dot(p_real, a_imag) + dot(p_imag, a_real)).astype(jnp.bfloat16)
        return here, real_part.reshape(group, span, columns), imag_part.reshape(group, span, columns)

    def renew(i):
        here, real_part, imag_part = contract(0, lax.rem(high + i, tiles))
        blocks1[here, 0:span] = real_part
        blocks1[here, span : 2 * span] = imag_part
        if i == 0:
            got1[me] = blocks1[me]
        over(i, lambda i, j: copy_to(1, i, j).start())

    got0[me] = blocks0[me]
    order = [2, 1, 3, 0]
    sends = [(i, j) for i in order for j in range(group) if i or j]
    ready = planes - 1 + 2 * steps * LAG
    entry = [c if c < planes else ready - EARLY + c - planes for c in range(chunks)]
    work = [functools.partial(absorb, 0, i) for i in order] + [functools.partial(renew, i) for i in order]
    unsent = list(order)
    total_slots = entry[-1] + 2 * steps * LAG + 1
    for t in range(total_slots):
        for c in range(chunks):
            if t < entry[c] or (t - entry[c]) % LAG:
                continue
            step = (t - entry[c]) // LAG
            if 1 <= step <= 2 * steps:
                finish(c, step - 1)
            if step < 2 * steps:
                begin(c, step)
        if unsent and t % max(1, int(ready * SPREAD) // tiles) == 0:
            over(unsent.pop(0), lambda i, j: copy_to(0, i, j).start())
        if t >= ready:
            assert not unsent
            for job in work[:UNITS]:
                job()
            work = work[UNITS:]
    assert not work

    for i in order:
        absorb(1, i)
    for where in range(tiles):
        here, real_part, imag_part = contract(1, where)
        out[0, here] = real_part
        out[1, here] = imag_part

    for r in range(2):
        for i in order:
            over(i, lambda i, j: copy_to(r, i, j).wait_send())
    for c in range(chunks):
        for s in range(steps):
            reduce_copy(c, s).wait_send()
            gather_copy(c, s, starts[s + 1]).wait_send()


def contract_network(n, part0, part1, blocks):
    planes, _, span, columns = part0.shape
    steps = n.bit_length() - 1
    both = (2 * planes,) + part0.shape[1:]
    vmem = pl.BlockSpec(memory_space=pltpu.VMEM)
    return pl.pallas_call(
        functools.partial(network_kernel, n),
        out_shape=jax.ShapeDtypeStruct((2, n, span, columns), jnp.bfloat16),
        in_specs=[vmem, vmem, vmem],
        out_specs=vmem,
        scratch_shapes=[
            pltpu.VMEM(both, jnp.float32),
            pltpu.VMEM(both, jnp.bfloat16),
            pltpu.VMEM(both, jnp.bfloat16),
            pltpu.VMEM(both, jnp.bfloat16),
            pltpu.VMEM(blocks.shape, jnp.bfloat16),
            pltpu.VMEM(blocks.shape, jnp.bfloat16),
            pltpu.VMEM(blocks.shape, jnp.bfloat16),
            pltpu.VMEM((2, n, span, columns), jnp.bfloat16),
            pltpu.SemaphoreType.DMA((2, n)),
            pltpu.SemaphoreType.DMA((2, n)),
            pltpu.SemaphoreType.DMA((2 * planes, 2 * steps)),
            pltpu.SemaphoreType.DMA((2 * planes, 2 * steps)),
        ],
        compiler_params=pltpu.CompilerParams(collective_id=0, has_side_effects=True),
    )(part0, part1, blocks)


def leaf_kernel(bits, left_ref, right_ref, out_ref):
    depth, row_count = left_ref.shape[2], left_ref.shape[4]
    width = right_ref.shape[4]
    left = left_ref[0, 0].reshape(2 * depth, row_count)
    right = right_ref[0, 0].reshape(2 * depth, width).astype(jnp.float32)
    even = lax.rem(lax.broadcasted_iota(jnp.int32, right.shape, 0), 2) == 0
    signed = jnp.where(even, right, -right).astype(jnp.bfloat16)
    swapped = jnp.where(even, pltpu.roll(right, 2 * depth - 1, 0), pltpu.roll(right, 1, 0)).astype(jnp.bfloat16)
    def product(a, b):
        return lax.dot_general(a, b, (((0,), (0,)), ((), ())), preferred_element_type=jnp.float32)

    @pl.when(pl.program_id(0) == 0)
    def _():
        out_ref[0, 0] = product(signed, left)
        out_ref[0, 1] = product(swapped, left)

    @pl.when(pl.program_id(0) != 0)
    def _():
        out_ref[0, 0] = product(left, signed)
        out_ref[0, 1] = product(left, swapped)


def leaf_terms(bits, leaf_left, leaf_right, first):
    _, _, depth, _, row_count = leaf_left.shape
    width = leaf_right.shape[4]

    def chosen(j, chosen_bits):
        return (first + j, chosen_bits[first + j], 0, 0, 0)

    return pl.pallas_call(
        leaf_kernel,
        out_shape=jax.ShapeDtypeStruct((2, 2, row_count, width), jnp.float32),
        grid_spec=pltpu.PrefetchScalarGridSpec(
            num_scalar_prefetch=1,
            grid=(2,),
            in_specs=[
                pl.BlockSpec((1, 1, depth, 2, row_count), chosen),
                pl.BlockSpec((1, 1, depth, 2, width), chosen),
            ],
            out_specs=pl.BlockSpec((1, 2, row_count, width), lambda j, chosen_bits: (j, 0, 0, 0)),
        ),
    )(bits, leaf_left, leaf_right)


def on_device(n, stem_tensor, leaf_left, leaf_right, slice_bits):
    width, columns = stem_tensor.shape[1], stem_tensor.shape[3]
    span = width // n
    blocks = jnp.transpose(stem_tensor.reshape(n, span, 2, columns), (0, 2, 1, 3)).reshape(n, 2 * span, columns)
    parts = [
        leaf_terms(slice_bits, leaf_left, leaf_right, 2 * r).reshape(PLANES, n, span, columns) for r in range(ROUNDS)
    ]
    state = contract_network(n, *parts, blocks).reshape(2, width, columns)
    return jnp.transpose(state, (1, 0, 2))[None]


def solution(mesh):
    return jax.shard_map(
        functools.partial(on_device, mesh.shape["outer"]),
        mesh=mesh,
        in_specs=(
            P(("cuts", "outer"), None, None, None),
            P(None, None, "outer", None, None),
            P(None, None, "outer", None, None),
            P("cuts"),
        ),
        out_specs=P(("cuts", "outer"), None, None, None),
        check_vma=False,
    )
```

```python
import functools

import jax
import jax.numpy as jnp
from jax import lax
from jax.experimental import pallas as pl
from jax.experimental.pallas import tpu as pltpu
from jax.sharding import PartitionSpec as P

ROUNDS = 2
TILES = 4
LAG = 2
EARLY = 12
SPREAD = 0.4
UNITS = 4
MESH = pl.DeviceIdType.MESH


def network_kernel(
    n, part, blocks0, out, acc, outgoing, incoming, branch, got0, got1, blocks1, absorbed,
    a_send, a_recv, r_send, r_recv,
):
    chunks, _, span, columns = part.shape
    planes = chunks // ROUNDS
    width = n * span
    steps = n.bit_length() - 1
    tiles = TILES
    group = n // tiles
    me = lax.axis_index("outer")
    high, low = me // group, lax.rem(me, group)

    barrier = pltpu.get_barrier_semaphore()

    def greet(k, carry):
        pl.semaphore_signal(barrier, inc=1, device_id={"outer": lax.rem(me + k, n)}, device_id_type=MESH)
        return carry

    lax.fori_loop(1, n, greet, 0)
    pl.semaphore_wait(barrier, n - 1)

    bits = [lax.rem(me // (1 << s), 2) for s in range(steps)]
    peers = [me + (1 << s) * (1 - 2 * bits[s]) for s in range(steps)]
    starts = [0]
    gives = []
    for s in range(steps):
        half = n >> (s + 1)
        gives.append(starts[s] + (1 - bits[s]) * half)
        starts.append(starts[s] + bits[s] * half)

    def copy_to(r, i, j):
        to = lax.rem(high + i, tiles) * group + lax.rem(low + j, group)
        k = i * group + j
        blocks, got = ((blocks0, got0), (blocks1, got1))[r]
        return pltpu.make_async_remote_copy(
            src_ref=blocks.at[to], dst_ref=got.at[me], send_sem=a_send.at[r, k], recv_sem=a_recv.at[r, k],
            device_id={"outer": to}, device_id_type=MESH)

    def copy_from(r, i, j):
        origin = lax.rem(high + tiles - i, tiles) * group + lax.rem(low + group - j, group)
        k = i * group + j
        blocks, got = ((blocks0, got0), (blocks1, got1))[r]
        return pltpu.make_async_remote_copy(
            src_ref=blocks.at[origin], dst_ref=got.at[origin], send_sem=a_send.at[r, k], recv_sem=a_recv.at[r, k],
            device_id={"outer": origin}, device_id_type=MESH)

    def over(i, act):
        def one(j, carry):
            act(i, j)
            return carry

        lax.fori_loop(1 if i == 0 else 0, group, one, 0)

    def reduce_copy(c, s):
        half, at = n >> (s + 1), n - (n >> s)
        return pltpu.make_async_remote_copy(
            src_ref=outgoing.at[c, pl.ds(gives[s], half)], dst_ref=incoming.at[c, pl.ds(at, half)],
            send_sem=r_send.at[c, s], recv_sem=r_recv.at[c, s],
            device_id={"outer": peers[s]}, device_id_type=MESH)

    def gather_copy(c, s, first):
        here = branch.at[c, pl.ds(first, n >> (s + 1))]
        return pltpu.make_async_remote_copy(
            src_ref=here, dst_ref=here, send_sem=r_send.at[c, 2 * steps - 1 - s], recv_sem=r_recv.at[c, 2 * steps - 1 - s],
            device_id={"outer": peers[s]}, device_id_type=MESH)

    def begin(c, step):
        if step < steps:
            give = pl.ds(gives[step], n >> (step + 1))
            source = acc if step else part
            outgoing[c, give] = source[c, give].astype(outgoing.dtype)
            reduce_copy(c, step).start()
        else:
            s = 2 * steps - 1 - step
            gather_copy(c, s, starts[s + 1]).start()

    def finish(c, step):
        if step < steps:
            half, at = n >> (step + 1), n - (n >> step)
            reduce_copy(c, step).wait_recv()
            keep = pl.ds(starts[step + 1], half)
            source = acc if step else part
            total = source[c, keep] + incoming[c, pl.ds(at, half)].astype(jnp.float32)
            if step == steps - 1:
                branch[c, keep] = total.astype(branch.dtype)
            else:
                acc[c, keep] = total
        else:
            s = 2 * steps - 1 - step
            gather_copy(c, s, gives[s]).wait_recv()

    def dot(a, b):
        return jnp.dot(a, b, preferred_element_type=jnp.float32)

    def absorb(r, i):
        got = (got0, got1)[r]
        over(i, lambda i, j: copy_from(r, i, j).wait_recv())
        here = pl.ds(lax.rem(high + tiles - i, tiles) * group, group)
        entries = got[here].reshape(group * 2 * span, columns)
        first = r * planes
        by_real = dot(entries, branch[first + 2].reshape(width, columns)).reshape(group, 2, span, columns)
        by_imag = dot(entries, branch[first + 3].reshape(width, columns)).reshape(group, 2, span, columns)
        absorbed[0, here] = (by_real[:, 0] - by_imag[:, 1]).astype(absorbed.dtype)
        absorbed[1, here] = (by_imag[:, 0] + by_real[:, 1]).astype(absorbed.dtype)

    def contract(r, where):
        here = pl.ds(where * group, group)
        first = r * planes
        p_real = branch[first, here].reshape(group * span, width)
        p_imag = branch[first + 1, here].reshape(group * span, width)
        a_real, a_imag = absorbed[0].reshape(width, columns), absorbed[1].reshape(width, columns)
        real_part = (dot(p_real, a_real) - dot(p_imag, a_imag)).astype(jnp.bfloat16)
        imag_part = (dot(p_real, a_imag) + dot(p_imag, a_real)).astype(jnp.bfloat16)
        return here, real_part.reshape(group, span, columns), imag_part.reshape(group, span, columns)

    def renew(i):
        here, real_part, imag_part = contract(0, lax.rem(high + i, tiles))
        blocks1[here, 0:span] = real_part
        blocks1[here, span : 2 * span] = imag_part
        if i == 0:
            got1[me] = blocks1[me]
        over(i, lambda i, j: copy_to(1, i, j).start())

    got0[me] = blocks0[me]
    order = [2, 1, 3, 0]
    sends = [(i, j) for i in order for j in range(group) if i or j]
    ready = planes - 1 + 2 * steps * LAG
    turn = [(c + planes // 2) % planes for c in range(planes)]
    entry = turn + [max(planes, ready - EARLY) + at for at in turn]
    work = [functools.partial(absorb, 0, i) for i in order] + [functools.partial(renew, i) for i in order]
    unsent = list(order)
    total_slots = max(entry) + 2 * steps * LAG + 1
    for t in range(total_slots):
        for c in range(chunks):
            if t < entry[c] or (t - entry[c]) % LAG:
                continue
            step = (t - entry[c]) // LAG
            if 1 <= step <= 2 * steps:
                finish(c, step - 1)
            if step < 2 * steps:
                begin(c, step)
        if unsent and t % max(1, int(ready * SPREAD) // tiles) == 0:
            over(unsent.pop(0), lambda i, j: copy_to(0, i, j).start())
        if t >= ready:
            assert not unsent
            for job in work[:UNITS]:
                job()
            work = work[UNITS:]
    assert not work

    for i in order:
        absorb(1, i)
    for where in range(tiles):
        here, real_part, imag_part = contract(1, where)
        out[0, here] = real_part
        out[1, here] = imag_part

    for r in range(2):
        for i in order:
            over(i, lambda i, j: copy_to(r, i, j).wait_send())
    for c in range(chunks):
        for s in range(steps):
            reduce_copy(c, s).wait_send()
            gather_copy(c, s, starts[s + 1]).wait_send()


def contract_network(n, part, blocks):
    chunks, _, span, columns = part.shape
    steps = n.bit_length() - 1
    both = part.shape
    vmem = pl.BlockSpec(memory_space=pltpu.VMEM)
    return pl.pallas_call(
        functools.partial(network_kernel, n),
        out_shape=jax.ShapeDtypeStruct((2, n, span, columns), jnp.bfloat16),
        in_specs=[vmem, vmem],
        out_specs=vmem,
        scratch_shapes=[
            pltpu.VMEM(both, jnp.float32),
            pltpu.VMEM(both, jnp.bfloat16),
            pltpu.VMEM(both, jnp.bfloat16),
            pltpu.VMEM(both, jnp.bfloat16),
            pltpu.VMEM(blocks.shape, jnp.bfloat16),
            pltpu.VMEM(blocks.shape, jnp.bfloat16),
            pltpu.VMEM(blocks.shape, jnp.bfloat16),
            pltpu.VMEM((2, n, span, columns), jnp.bfloat16),
            pltpu.SemaphoreType.DMA((2, n)),
            pltpu.SemaphoreType.DMA((2, n)),
            pltpu.SemaphoreType.DMA((chunks, 2 * steps)),
            pltpu.SemaphoreType.DMA((chunks, 2 * steps)),
        ],
        compiler_params=pltpu.CompilerParams(collective_id=0, has_side_effects=True),
    )(part, blocks)


def leaf_product(plain_ref, other_ref, out_ref):
    rows = 2 * plain_ref.shape[2]
    plain = plain_ref[0, 0].reshape(rows, plain_ref.shape[4])
    other = other_ref[0, 0].reshape(rows, other_ref.shape[4]).astype(jnp.float32)
    even = lax.rem(lax.broadcasted_iota(jnp.int32, other.shape, 0), 2) == 0
    signed = jnp.where(even, other, -other).astype(jnp.bfloat16)
    swapped = jnp.where(even, pltpu.roll(other, rows - 1, 0), pltpu.roll(other, 1, 0)).astype(jnp.bfloat16)
    dims = (((0,), (0,)), ((), ()))
    out_ref[0, 0] = lax.dot_general(plain, signed, dims, preferred_element_type=jnp.float32)
    out_ref[0, 1] = lax.dot_general(plain, swapped, dims, preferred_element_type=jnp.float32)


def leaf_kernel(bits, left_ref, right_ref, out_ref):
    transposed = lax.rem(pl.program_id(0), 2) == 0

    @pl.when(transposed)
    def _():
        leaf_product(right_ref, left_ref, out_ref)

    @pl.when(jnp.logical_not(transposed))
    def _():
        leaf_product(left_ref, right_ref, out_ref)


def leaf_terms(bits, leaf_left, leaf_right):
    branches, _, depth, _, row_count = leaf_left.shape
    width = leaf_right.shape[4]

    def chosen(j, chosen_bits):
        return (j, chosen_bits[j], 0, 0, 0)

    return pl.pallas_call(
        leaf_kernel,
        out_shape=jax.ShapeDtypeStruct((branches, 2, row_count, width), jnp.float32),
        grid_spec=pltpu.PrefetchScalarGridSpec(
            num_scalar_prefetch=1,
            grid=(branches,),
            in_specs=[
                pl.BlockSpec((1, 1, depth, 2, row_count), chosen),
                pl.BlockSpec((1, 1, depth, 2, width), chosen),
            ],
            out_specs=pl.BlockSpec((1, 2, row_count, width), lambda j, chosen_bits: (j, 0, 0, 0)),
        ),
    )(bits, leaf_left, leaf_right)


def on_device(n, stem_tensor, leaf_left, leaf_right, slice_bits):
    width, columns = stem_tensor.shape[1], stem_tensor.shape[3]
    span = width // n
    blocks = jnp.transpose(stem_tensor.reshape(n, span, 2, columns), (0, 2, 1, 3)).reshape(n, 2 * span, columns)
    part = leaf_terms(slice_bits, leaf_left, leaf_right).reshape(-1, n, span, columns)
    state = contract_network(n, part, blocks).reshape(2, width, columns)
    return jnp.transpose(state, (1, 0, 2))[None]


def solution(mesh):
    return jax.shard_map(
        functools.partial(on_device, mesh.shape["outer"]),
        mesh=mesh,
        in_specs=(
            P(("cuts", "outer"), None, None, None),
            P(None, None, "outer", None, None),
            P(None, None, "outer", None, None),
            P("cuts"),
        ),
        out_specs=P(("cuts", "outer"), None, None, None),
        check_vma=False,
    )
```
